32 devices in a mesh: row: 4 (over y, core), col: 2 (over x), layer: 4 (over z).
Axes of the slice: x: 2, y: 2, z: 4, core: 2. Of those that a mesh axis runs over, the one named last changes fastest.
Arguments:
- density: bfloat16 [8192, 4, 2048], P('row', 'layer', 'col'), may hold values from -6 to 6
- response: bfloat16 [4, 2048, 8192], P('layer', 'row', 'col'), may hold values from -0.125 to 0.125
- density_mask: int32 [64, 4, 16], P('row', 'layer', 'col'), may hold values 0 or 1
- response_mask: int32 [4, 16, 64], P('layer', 'row', 'col'), may hold values 0 or 1
- result_mask: int32 [64, 64], P('row', 'col'), may hold values 0 or 1
Outputs:
- perturbed: bfloat16 [16, 2, 256, 8192], P(('row', 'layer'), 'col')
The draws below stay inside these ranges and needn't reach their ends.
All inputs are finite; a program needn't handle non-finite values. No bound on the sum of `density_mask` or of `response_mask` or of `result_mask` on one device may be relied on, other than what follows from the above.
Results may differ from the reference program's by a relative error of at most 0.0042.
Values may be sent and summed in bfloat16 or wider, within the bound.
A program may use at most 192 MiB of HBM per device.

```python
import jax
import jax.numpy as jnp

ORDER = 8192
NBLK = 64
BANDS = 16
SLAB = 256
N_COL = 2
N_LAYER = 4


def with_ends(entries, key, low, high):
    longest = entries.shape.index(max(entries.shape))
    spots = []
    for shift in (0, 1):
        where = [jax.random.randint(jax.random.fold_in(key, axis), (), 0, length) for axis, length in enumerate(entries.shape)]
        where[longest] = (where[longest] + shift) % entries.shape[longest]
        spots.append(tuple(where))
    return entries.at[spots[0]].set(low).at[spots[1]].set(high)


def shard_levels(own_key, extent, split, least, top_value):
    def one(dim, blocks):
        heights = jax.random.uniform(jax.random.fold_in(jax.random.fold_in(own_key, 6), dim), (blocks,), jnp.float32, least / len(split), top_value / len(split))
        return jnp.repeat(jnp.exp(heights), extent[dim] // blocks).reshape((-1,) + (1,) * (len(extent) - dim - 1))

    level = one(*split[0])
    for cut in split[1:]:
        level = level * one(*cut)
    return level


def scatter_about(own_key, shape, spread, reach, cuts=(), held_as=jnp.bfloat16):
    result = spread * jax.random.normal(own_key, shape, jnp.float32)
    if cuts:
        result = result * shard_levels(own_key, shape, cuts, -0.22, 0.18)
    return jnp.clip(result, -reach, reach).astype(held_as)


def setup_inputs(seed: int = 0) -> dict:
    streams_of = jax.random.split(jax.random.key(seed), 6)
    density = scatter_about(streams_of[0], (ORDER, N_LAYER, ORDER // N_LAYER), 1.0, 6.0, ((0, 4), (1, 4), (2, 2)))
    response = scatter_about(streams_of[1], (N_LAYER, ORDER // N_LAYER, ORDER), (ORDER // 4) ** -0.5, 0.125, ((0, 4), (1, 4), (2, 2)))
    density_mask = with_ends((jax.random.randint(streams_of[2], (NBLK, N_LAYER, NBLK // N_LAYER), 0, 2) < 1).astype(jnp.int32), jax.random.fold_in(streams_of[2], 1), 0, 1)
    response_mask = with_ends((jax.random.randint(streams_of[3], (N_LAYER, NBLK // N_LAYER, NBLK), 0, 2) < 1).astype(jnp.int32), jax.random.fold_in(streams_of[3], 1), 0, 1)
    result_mask = with_ends((jax.random.randint(streams_of[4], (NBLK, NBLK), 0, 2) < 1).astype(jnp.int32), jax.random.fold_in(streams_of[4], 1), 0, 1)
    return {"density": density, "response": response, "density_mask": density_mask, "response_mask": response_mask, "result_mask": result_mask}


def expand_mask(values, pattern):
    height, breadth = values.shape
    block_rows, block_cols = pattern.shape
    shaped = values.reshape(block_rows, height // block_rows, block_cols, breadth // block_cols)
    masked = shaped * pattern[:, None, :, None].astype(values.dtype)
    return masked.reshape(height, breadth)


def reference(density, response, density_mask, response_mask, result_mask):
    left = expand_mask(density.reshape(ORDER, ORDER), density_mask.reshape(NBLK, NBLK))
    right = expand_mask(response.reshape(ORDER, ORDER), response_mask.reshape(NBLK, NBLK))
    product = jnp.dot(left, right, preferred_element_type=jnp.float32)
    product = expand_mask(product, result_mask).astype(jnp.bfloat16)
    widened = product.astype(jnp.float32)
    summed = (widened + widened.T).astype(jnp.bfloat16)
    return summed.reshape(BANDS, N_COL, SLAB, ORDER)
```

```python
import jax
import jax.numpy as jnp
from jax import lax
from jax.sharding import PartitionSpec as P

CHUNKS = 2


def expand_mask(values, pattern):
    height, breadth = values.shape
    block_rows, block_cols = pattern.shape
    shaped = values.reshape(block_rows, height // block_rows, block_cols, breadth // block_cols)
    masked = shaped * pattern[:, None, :, None].astype(values.dtype)
    return masked.reshape(height, breadth)


def swap(values, axis):
    return lax.ppermute(values, axis, [(0, 1), (1, 0)])


def in_order(mine, other, position, axis):
    return jnp.where(
        position == 0,
        jnp.concatenate([mine, other], axis=axis),
        jnp.concatenate([other, mine], axis=axis),
    )


def line_reduce_scatter(partial, axis):
    count = lax.axis_size(axis)
    here = lax.axis_index(axis)
    height = partial.shape[0] // count

    def band(index):
        index = jnp.clip(index, 0, count - 1)
        return lax.dynamic_slice_in_dim(partial, index * height, height, 0)

    up = down = None
    for step in range(count - 1):
        ahead = count - 1 - step
        to_up, to_down = band(here + ahead), band(here - ahead)
        if step:
            to_up = to_up + up.astype(jnp.float32)
            to_down = to_down + down.astype(jnp.float32)
        up = lax.ppermute(to_up.astype(jnp.bfloat16), axis, [(i, i + 1) for i in range(step + 1)])
        down = lax.ppermute(
            to_down.astype(jnp.bfloat16), axis, [(count - 1 - i, count - 2 - i) for i in range(step + 1)]
        )
    total = band(here)
    if count > 1:
        total = total + up.astype(jnp.float32) + down.astype(jnp.float32)
    return total.astype(jnp.bfloat16)


def per_device(density, response, density_mask, response_mask, result_mask):
    columns = lax.axis_size("col")
    layers = lax.axis_size("layer")
    place = lax.axis_index("col")
    paired = columns == 2
    right = response.reshape(response.shape[1], response.shape[2])
    right_mask = response_mask.reshape(response_mask.shape[1], response_mask.shape[2])
    left = expand_mask(
        density.reshape(density.shape[0], density.shape[2]),
        density_mask.reshape(density_mask.shape[0], density_mask.shape[2]),
    )
    breadth = right.shape[1]
    band_rows = left.shape[0] // layers
    slab_rows = band_rows // columns
    order_total = breadth * columns
    chunks = CHUNKS if breadth % (CHUNKS * columns * slab_rows) == 0 and right_mask.shape[1] % CHUNKS == 0 else 1
    width = breadth // chunks
    mask_width = right_mask.shape[1] // chunks

    if paired:
        left = in_order(left, swap(left, "col"), place, 1)
    else:
        left = lax.all_gather(left, "col", axis=1, tiled=True)

    own_mine, own_other, mirror_mine, mirror_other = [], [], [], []
    for chunk in range(chunks):
        piece = expand_mask(
            right[:, chunk * width : (chunk + 1) * width],
            right_mask[:, chunk * mask_width : (chunk + 1) * mask_width],
        )
        panel = lax.all_gather(piece, "row", axis=0, tiled=True)
        partial = jnp.dot(left, panel, preferred_element_type=jnp.float32)
        partial = expand_mask(partial, result_mask[:, chunk * mask_width : (chunk + 1) * mask_width])
        block = line_reduce_scatter(partial, "layer")
        groups = width // (columns * slab_rows)
        slabs = block.reshape(columns, slab_rows, width)
        flipped = block.reshape(band_rows, groups, columns, slab_rows)
        if paired:
            own_mine.append(lax.dynamic_index_in_dim(slabs, place, 0, False))
            own_other.append(swap(lax.dynamic_index_in_dim(slabs, 1 - place, 0, False), "col"))
            mirror_mine.append(lax.dynamic_index_in_dim(flipped, place, 2, False).transpose(1, 2, 0))
            mirror_other.append(
                swap(lax.dynamic_index_in_dim(flipped, 1 - place, 2, False).transpose(1, 2, 0), "col")
            )
        else:
            own_mine.append(
                lax.all_to_all(slabs, "col", split_axis=0, concat_axis=0, tiled=True).reshape(columns, slab_rows, width)
            )
            mirror_mine.append(
                lax.all_to_all(
                    flipped.transpose(2, 1, 3, 0), "col", split_axis=0, concat_axis=0, tiled=True
                )
            )
    if paired:
        own = in_order(jnp.concatenate(own_mine, 1), jnp.concatenate(own_other, 1), place, 1)
        mirror = in_order(jnp.concatenate(mirror_mine, 0), jnp.concatenate(mirror_other, 0), place, 0)
    else:
        own = jnp.concatenate(own_mine, 2).transpose(1, 0, 2).reshape(slab_rows, order_total)
        mirror = jnp.concatenate(mirror_mine, 1).reshape(-1, slab_rows, band_rows)
    mirror = lax.all_to_all(mirror, ("row", "layer"), split_axis=0, concat_axis=0, tiled=True)
    mirror = mirror.transpose(1, 0, 2).reshape(slab_rows, order_total)
    result = (own.astype(jnp.float32) + mirror.astype(jnp.float32)).astype(jnp.bfloat16)
    return result.reshape(1, 1, slab_rows, order_total)


def solution(mesh):
    placed = (
        P("row", "layer", "col"),
        P("layer", "row", "col"),
        P("row", "layer", "col"),
        P("layer", "row", "col"),
        P("row", "col"),
    )
    return jax.shard_map(
        per_device,
        mesh=mesh,
        in_specs=placed,
        out_specs=P(("row", "layer"), "col", None, None),
        check_vma=False,
    )
```

```python
import jax
import jax.numpy as jnp
from jax import lax
from jax.experimental.layout import Layout, with_layout_constraint
from jax.sharding import PartitionSpec as P

CHUNKS = 2


def expand_mask(values, pattern):
    height, breadth = values.shape
    block_rows, block_cols = pattern.shape
    wide = jnp.repeat(pattern.astype(values.dtype), breadth // block_cols, axis=1)
    wide = lax.optimization_barrier(wide)
    masked = values.reshape(block_rows, height // block_rows, breadth) * wide[:, None, :]
    return masked.reshape(height, breadth)


def pinned(values):
    return with_layout_constraint(values, Layout(major_to_minor=tuple(range(values.ndim))))


def swap(values, axis):
    return lax.ppermute(values, axis, [(0, 1), (1, 0)])


def in_order(mine, other, position, axis):
    return jnp.where(
        position == 0,
        jnp.concatenate([mine, other], axis=axis),
        jnp.concatenate([other, mine], axis=axis),
    )


def line_reduce_scatter(partial, axis, held=None, at=None):
    count = lax.axis_size(axis)
    here = lax.axis_index(axis)
    height = partial.shape[0] // count

    def band(index):
        index = jnp.clip(index, 0, count - 1)
        return lax.dynamic_slice_in_dim(partial, index * height, height, 0)

    up = down = None
    for step in range(count - 1):
        ahead = count - 1 - step
        to_up, to_down = band(here + ahead), band(here - ahead)
        if step:
            to_up = to_up + up.astype(jnp.float32)
            to_down = to_down + down.astype(jnp.float32)
        up = lax.ppermute(to_up.astype(jnp.bfloat16), axis, [(i, i + 1) for i in range(step + 1)])
        down = lax.ppermute(
            to_down.astype(jnp.bfloat16), axis, [(count - 1 - i, count - 2 - i) for i in range(step + 1)]
        )
        if held is not None and step == at:
            up, down, held = lax.optimization_barrier((up, down, held))
    total = band(here)
    if count > 1:
        total = total + up.astype(jnp.float32) + down.astype(jnp.float32)
    return total.astype(jnp.bfloat16), held


def per_device(density, response, density_mask, response_mask, result_mask):
    columns = lax.axis_size("col")
    layers = lax.axis_size("layer")
    place = lax.axis_index("col")
    paired = columns == 2
    right = response.reshape(response.shape[1], response.shape[2])
    right_mask = response_mask.reshape(response_mask.shape[1], response_mask.shape[2])
    left = density.reshape(density.shape[0], density.shape[2])
    left_mask = density_mask.reshape(density_mask.shape[0], density_mask.shape[2])
    breadth = right.shape[1]
    band_rows = left.shape[0] // layers
    slab_rows = band_rows // columns
    order_total = breadth * columns
    mask_rows = left_mask.shape[0] // layers
    slabs = columns if paired and mask_rows % columns == 0 else 1
    mask_cols = right_mask.shape[1]
    chunks = CHUNKS if breadth % (CHUNKS * columns * slab_rows) == 0 and mask_cols % CHUNKS == 0 else 1
    width = breadth // chunks
    mask_width = mask_cols // chunks

    def rows_of(values, slab):
        split = values.reshape(layers, slabs, -1, values.shape[1])
        return split[:, slab].reshape(-1, values.shape[1])

    def left_of(slab):
        mine = expand_mask(rows_of(left, slab), rows_of(left_mask, slab))
        if paired:
            return in_order(mine, swap(mine, "col"), place, 1)
        return lax.all_gather(mine, "col", axis=1, tiled=True)

    def panel_of(chunk):
        piece = expand_mask(
            right[:, chunk * width : (chunk + 1) * width],
            right_mask[:, chunk * mask_width : (chunk + 1) * mask_width],
        )
        return lax.all_gather(piece, "row", axis=0, tiled=True)

    panels = [panel_of(chunk) for chunk in range(chunks)]
    lefts = [left_of(slab) for slab in range(slabs)]
    groups = width // (columns * slab_rows)
    own, mirrors = [], []
    for slab in range(slabs):
        blocks, sent, mirror_mine, mirror_other = [], [], [], []
        for chunk in range(chunks):
            partial = jnp.dot(lefts[slab], panels[chunk], preferred_element_type=jnp.float32)
            kept = rows_of(result_mask, slab)[:, chunk * mask_width : (chunk + 1) * mask_width]
            partial = expand_mask(partial, kept)
            if slab == 0 and chunk == 0 and chunks > 1:
                block, panels[1] = line_reduce_scatter(partial, "layer", panels[1], layers - 3)
            elif slab == slabs - 1 and chunk and slabs > 1:
                block, sent[-1] = line_reduce_scatter(partial, "layer", sent[-1], layers - 2)
            else:
                block, _ = line_reduce_scatter(partial, "layer")
            blocks.append(block)
            if slabs > 1:
                sent.append(lax.ppermute(block, "col", [(1 - slab, slab)]))
            flipped = block.reshape(-1, groups, columns, slab_rows)
            if paired:
                keep = lax.dynamic_index_in_dim(flipped, place, 2, False).transpose(1, 2, 0)
                send = lax.dynamic_index_in_dim(flipped, 1 - place, 2, False).transpose(1, 2, 0)
                mirror_mine.append(pinned(keep))
                mirror_other.append(swap(pinned(send), "col"))
            else:
                flipped = flipped.transpose(2, 1, 3, 0)
                mirror_mine.append(lax.all_to_all(flipped, "col", split_axis=0, concat_axis=0, tiled=True))
        if slabs > 1:
            own.append(in_order(jnp.concatenate(blocks, 1), jnp.concatenate(sent, 1), place, 1))
        else:
            whole = jnp.concatenate(blocks, 1).reshape(columns, slab_rows, breadth)
            whole = lax.all_to_all(whole, "col", split_axis=0, concat_axis=0, tiled=True)
            own.append(whole.reshape(columns, slab_rows, breadth).transpose(1, 0, 2).reshape(slab_rows, order_total))
        if paired:
            mirror = in_order(jnp.concatenate(mirror_mine, 0), jnp.concatenate(mirror_other, 0), place, 0)
        else:
            mirror = jnp.concatenate(mirror_mine, 1).reshape(-1, slab_rows, band_rows)
        mirrors.append(lax.all_to_all(mirror, ("row", "layer"), split_axis=0, concat_axis=0, tiled=True))
    own_band = jnp.where(place == 0, own[0], own[-1])
    mirrored = pinned(jnp.concatenate(mirrors, 2).transpose(1, 0, 2).reshape(slab_rows, order_total))
    result = (own_band.astype(jnp.float32) + mirrored.astype(jnp.float32)).astype(jnp.bfloat16)
    return result.reshape(1, 1, slab_rows, order_total)


def solution(mesh):
    placed = (
        P("row", "layer", "col"),
        P("layer", "row", "col"),
        P("row", "layer", "col"),
        P("layer", "row", "col"),
        P("row", "col"),
    )
    return jax.shard_map(
        per_device,
        mesh=mesh,
        in_specs=placed,
        out_specs=P(("row", "layer"), "col", None, None),
        check_vma=False,
    )
```
